32 devices in a mesh: cells: 8 (over y, x, core), modes: 4 (over z).
Axes of the slice: x: 2, y: 2, z: 4, core: 2. Of those that a mesh axis runs over, the one named last changes fastest.
Arguments:
- phonons: float32 [8, 8, 8, 16, 6144], P('cells', None, None, None, 'modes'), may hold values from -6 to 6
- heaters: int32 [8, 8, 8, 16], P('cells'), may hold values 0 or 1
- courant: float32 [3, 6144], P(None, 'modes'), may hold values from 0.05 to 0.3
- upwind: int32 [3, 6144], P(None, 'modes'), may hold values from 0 to 1
- relaxation: float32 [6144], P('modes'), may hold values from 0.02 to 0.4
- source: float32 [6144], P('modes'), may hold values from -6 to 6
- coupling: bfloat16 [6144, 6144], P('modes'), may hold values from -0.0390625 to 0.0390625
Outputs:
- evolved: float32 [8, 8, 8, 16, 6144], P('cells', None, None, None, 'modes')
The draws below stay inside these ranges and needn't reach their ends.
All inputs are finite; a program needn't handle non-finite values. No bound on the sum of `heaters` on one device may be relied on, other than what follows from the above.
Results may differ from the reference program's by a relative error of at most 0.0018.
Values may be sent and summed in bfloat16 or wider, within the bound.
A program may use at most 128 MiB of HBM per device.

```python
import math
import jax
import jax.numpy as jnp
from jax import lax

MODES = 6144
GY = 4
CX = 8
CY = 8
CZ = 16
STEPS = 2
BLOCKS = 8


def with_ends(entries, key, low, high):
    longest = entries.shape.index(max(entries.shape))
    spots = []
    for shift in (0, 1):
        where = [jax.random.randint(jax.random.fold_in(key, axis), (), 0, length) for axis, length in enumerate(entries.shape)]
        where[longest] = (where[longest] + shift) % entries.shape[longest]
        spots.append(tuple(where))
    return entries.at[spots[0]].set(low).at[spots[1]].set(high)


def steps_of(rng, extent, pieces, smallest, top_value):
    def one(position, parts):
        draws = jax.random.uniform(jax.random.fold_in(jax.random.fold_in(rng, 6), position), (parts,), jnp.float32, smallest / len(pieces), top_value / len(pieces))
        return jnp.repeat(jnp.exp(draws), extent[position] // parts).reshape((-1,) + (1,) * (len(extent) - position - 1))

    level = one(*pieces[0])
    for cut in pieces[1:]:
        level = level * one(*cut)
    return level


def scatter_about(own_key, dims, spread, most, shards=(), dtype=jnp.bfloat16):
    loudness = steps_of(own_key, dims, shards, -0.22, 0.18) if shards else 1.0
    values = jax.random.normal(own_key, dims, jnp.float32) * spread * loudness
    return jnp.minimum(jnp.maximum(values, -most), most).astype(dtype)


def setup_inputs(seed: int = 0) -> dict:
    key_of = jax.random.split(jax.random.key(seed), 8)
    return {
        "phonons": scatter_about(key_of[0], (BLOCKS, CX, CY, CZ, MODES), 1.0, 6.0, ((0, 8), (4, 4)), jnp.float32),
        "heaters": with_ends((jax.random.randint(key_of[1], (BLOCKS, CX, CY, CZ), 0, 4) < 1).astype(jnp.int32), jax.random.fold_in(key_of[1], 1), 0, 1),
        "courant": jnp.clip(jnp.exp(math.log(0.3) - 1.7917595 * jax.random.uniform(key_of[2], (3, MODES), jnp.float32) ** steps_of(key_of[2], (3, MODES), ((1, 4),), -0.2, 0.2)), 0.05, 0.3),
        "upwind": with_ends(jax.random.randint(key_of[3], (3, MODES), 0, 2), jax.random.fold_in(key_of[3], 1), 0, 1).astype(jnp.int32),
        "relaxation": jnp.clip(jnp.exp(math.log(0.4) - 2.9957323 * jax.random.uniform(key_of[4], (MODES,), jnp.float32) ** steps_of(key_of[4], (MODES,), ((0, 4),), -0.2, 0.2)), 0.02, 0.4),
        "source": scatter_about(key_of[5], (MODES,), 1.0, 6.0, ((0, 4),), jnp.float32),
        "coupling": scatter_about(key_of[6], (MODES, MODES), (4 * MODES) ** -0.5, 0.0390625, ((0, 4),)),
    }


def to_grid(array, block_rows):
    placed = jnp.roll(array, 2, axis=0)
    shaped = placed.reshape((block_rows, GY) + array.shape[1:])
    order = (0, 2, 1, 3) + tuple(range(4, shaped.ndim))
    return shaped.transpose(order).reshape((block_rows * CX, GY * CY) + array.shape[3:])


def from_grid(grid, block_rows):
    shaped = grid.reshape((block_rows, CX, GY, CY) + grid.shape[2:])
    order = (0, 2, 1, 3) + tuple(range(4, shaped.ndim))
    blocks = shaped.transpose(order).reshape((block_rows * GY, CX, CY) + grid.shape[2:])
    return jnp.roll(blocks, -2, axis=0)


def upstream(density, forward, axis):
    widths = [(0, 0)] * density.ndim
    widths[axis] = (1, 1)
    padded = jnp.pad(density, widths)
    length_axis = density.shape[axis]
    behind = lax.slice_in_dim(padded, 0, length_axis, axis=axis)
    ahead = lax.slice_in_dim(padded, 2, length_axis + 2, axis=axis)
    return jnp.where(forward, behind, ahead)


def upstream_loop(density, forward, axis):
    behind = jnp.roll(density, 1, axis=axis)
    ahead = jnp.roll(density, -1, axis=axis)
    return jnp.where(forward, behind, ahead)


def reference(phonons, heaters, courant, upwind, relaxation, source, coupling):
    block_rows = phonons.shape[0] // GY
    density = to_grid(phonons, block_rows)
    heating = to_grid(heaters, block_rows).astype(jnp.float32)[..., None] * source
    widened = coupling.astype(jnp.float32)
    for repeat in range(STEPS):
        rounded = lax.optimization_barrier(density.astype(jnp.bfloat16)).astype(jnp.float32)
        scattered = jnp.dot(rounded.reshape(-1, MODES), widened.T, precision=lax.Precision.HIGHEST).reshape(density.shape)
        transport = courant[0] * (density - upstream_loop(density, upwind[0] == 1, 0))
        transport = transport + courant[1] * (density - upstream(density, upwind[1] == 1, 1))
        transport = transport + courant[2] * (density - upstream(density, upwind[2] == 1, 2))
        density = density - transport - relaxation * density - scattered + heating
    return from_grid(density, block_rows)
```

```python
import jax
import jax.numpy as jnp
from jax import lax
from jax.experimental import pallas as pl
from jax.experimental.pallas import tpu as pltpu
from jax.sharding import PartitionSpec as P

GY = 4
STEPS = 2

PLANES = 1
TILE = 256
LENT_AT = 5
MESH = pl.DeviceIdType.MESH


def line_kernel(phonons, heat, rates, coupling, out, dens, own, got, weights, old, facex, facey, total,
                load_sem, ss, rs, fys, fyr, fxs, fxr, hs, hr, out_sem):
    cell, me = lax.axis_index("cells"), lax.axis_index("modes")
    count = own.shape[0]
    steps_all = STEPS * count
    planes = count * PLANES
    ny, nz, width = own.shape[2:]
    rows = PLANES * ny * nz
    blocks = lax.axis_size("cells")
    half = me // 2
    inner = lax.rem((me + 1) // 2, 2)
    is_inner = inner == 1
    toward = 1 - 2 * half
    inward, outward = me + toward, me - toward
    near, far = me + 2 * toward, 3 - 3 * half
    y_next, y_last = lax.rem(cell + 1, blocks), lax.rem(cell + blocks - 1, blocks)
    x_next, x_last = lax.rem(cell + GY, blocks), lax.rem(cell + blocks - GY, blocks)
    twin = cell + 1 - 2 * lax.rem(cell, 2)
    flip2 = 2 - 4 * lax.rem(cell // 2, 2)
    flip4 = 4 - 8 * lax.rem(cell // 4, 2)
    peers = (cell + flip2, cell + flip4, cell + flip2 + flip4)
    column = lax.rem(lax.rem(cell + 2, blocks), GY)
    low_ok = jnp.where(column != 0, 1.0, 0.0).astype(jnp.float32)
    high_ok = jnp.where(column != GY - 1, 1.0, 0.0).astype(jnp.float32)

    def remote(src, dst, send, recv, c, m):
        return pltpu.make_async_remote_copy(
            src_ref=src, dst_ref=dst, send_sem=send, recv_sem=recv, device_id=(c, m), device_id_type=MESH
        )

    def own_in(i):
        return remote(own.at[lax.rem(i, count)], got.at[1 - inner, i], ss.at[0, i], rs.at[1 - inner, i], cell, inward)

    def own_out(i):
        return remote(own.at[lax.rem(i, count)], got.at[0, i], ss.at[1, i], rs.at[0, i], cell, outward)

    def relay(i):
        return remote(got.at[1, i], got.at[2, i], ss.at[2, i], rs.at[2, i], cell, inward)

    def part(i):
        return remote(got.at[1, i], got.at[2, i], ss.at[3, i], rs.at[2, i], cell, outward)

    def arrived(slot, i):
        remote(got.at[slot, i], got.at[slot, i], ss.at[0, i], rs.at[slot, i], cell, inward).wait_recv()

    def face_y(side, i):
        line = own.at[lax.rem(i, count), :, ny - 1 if side == 0 else 0]
        return remote(line, facey.at[side, i], fys.at[side, i], fyr.at[side, i], y_next if side == 0 else y_last, me)

    def face_x(side, s):
        plane = own.at[count - 1, PLANES - 1] if side == 0 else own.at[0, 0]
        return remote(plane, facex.at[side, s], fxs.at[side, s], fxr.at[side, s], x_next if side == 0 else x_last, me)

    share = width // blocks

    def lent_rows(c):
        return pl.ds(pl.multiple_of(c * share, share), share)

    def lent_z(k):
        block = near if k == 0 else far
        src = coupling.at[lent_rows(cell), pl.ds(pl.multiple_of(block * width, width), width)]
        return remote(src, weights.at[4 + k, lent_rows(cell)], hs.at[k], hr.at[k], cell, inward)

    def lent_peer(q, k):
        piece = weights.at[4 + k, lent_rows(cell)]
        return remote(piece, piece, hs.at[2 + 2 * q + k], hr.at[2 + 2 * q + k], peers[q], me)

    def lent_twin(q, k):
        piece = weights.at[4 + k, lent_rows(cell if q == 3 else peers[q])]
        return remote(piece, piece, hs.at[8 + 2 * q + k], hr.at[8 + 2 * q + k], twin, me)

    pairs = [(q, k) for q in range(3) for k in range(2)]
    twins = [(q, k) for q in range(4) for k in range(2)]

    def on_own_sends(i, act):
        act(own_in(i))
        pl.when(is_inner)(lambda: act(own_out(i)))
        act(face_y(0, i))
        act(face_y(1, i))
        pl.when(lax.rem(i, count) == 0)(lambda: act(face_x(1, i // count)))
        pl.when(lax.rem(i, count) == count - 1)(lambda: act(face_x(0, i // count)))

    def matrix(piece):
        return piece[...].reshape(rows, width)

    def product(piece, block, tile):
        weight = weights[block, pl.ds(pl.multiple_of(tile * TILE, TILE), TILE), :]
        return lax.dot_general(matrix(piece), weight, (((1,), (1,)), ((), ())), preferred_element_type=jnp.float32)

    def add_product(piece, block, first=False):
        @pl.loop(0, width // TILE)
        def _(tile):
            lanes = pl.ds(pl.multiple_of(tile * TILE, TILE), TILE)
            value = product(piece, block, tile)
            total[:, lanes] = value if first else total[:, lanes] + value

    def partial_sum(i):
        relay(i).wait_send()

        @pl.loop(0, width // TILE)
        def _(tile):
            lanes = pl.ds(pl.multiple_of(tile * TILE, TILE), TILE)
            value = product(got.at[0, i], 4, tile) + product(got.at[2, i], 5, tile)
            got[1, i, :, :, :, lanes] = value.astype(jnp.bfloat16).reshape(PLANES, ny, nz, TILE)

        part(i).start()

    def process(i):
        s, k = i // count, lax.rem(i, count)
        add_product(own.at[k], 0, True)
        arrived(0, i)
        add_product(got.at[0, i], 1)
        pl.when(is_inner)(lambda: add_product(got.at[1, i], 2))
        arrived(2, i)
        pl.when(is_inner)(lambda: add_product(got.at[2, i], 3))

        @pl.when(jnp.logical_not(is_inner))
        def _():
            total[...] = total[...] + got[2, i].reshape(rows, width).astype(jnp.float32)

        face_y(0, i).wait_recv()
        face_y(1, i).wait_recv()

        @pl.when(k == 0)
        def _():
            face_x(0, s).wait_recv()
            old[1, 1 : ny + 1] = facex[0, s].astype(jnp.float32)

        @pl.when(k == count - 1)
        def _():
            face_x(1, s).wait_recv()
            dens[planes] = facex[1, s].astype(jnp.float32)

        on_own_sends(i, lambda copy: copy.wait_send())
        spot = lax.broadcasted_iota(jnp.int32, (nz, 512), 0)
        for p in range(PLANES):
            plane = k * PLANES + p
            cur = lax.rem(plane, 2)
            old[cur, 1 : ny + 1] = dens[plane]
            old[cur, 0] = facey[0, i, p].astype(jnp.float32) * low_ok
            old[cur, ny + 1] = facey[1, i, p].astype(jnp.float32) * high_ok

            @pl.loop(0, ny)
            def _(y):
                warm = heat[plane, pl.ds(pl.multiple_of(y * nz, nz), nz), :]
                for lane in range(0, width, 512):
                    lanes = slice(lane, lane + 512)
                    here = old[cur, y + 1, :, lanes]
                    new = rates[0:1, lanes] * here
                    new += rates[1:2, lanes] * old[1 - cur, y + 1, :, lanes]
                    new += rates[2:3, lanes] * dens[plane + 1, y, :, lanes]
                    new += rates[3:4, lanes] * old[cur, y, :, lanes]
                    new += rates[4:5, lanes] * old[cur, y + 2, :, lanes]
                    new += rates[5:6, lanes] * jnp.where(spot == 0, 0.0, pltpu.roll(here, 1, 0))
                    new += rates[6:7, lanes] * jnp.where(spot == nz - 1, 0.0, pltpu.roll(here, nz - 1, 0))
                    line = pl.ds(pl.multiple_of((p * ny + y) * nz, nz), nz)
                    new += warm * rates[7:8, lanes] - total[line, lanes]
                    dens[plane, y, :, lanes] = new
                    own[k, p, y, :, lanes] = new.astype(jnp.bfloat16)

        pl.when(s < STEPS - 1)(lambda: on_own_sends(i + count, lambda copy: copy.start()))
        pl.when(s == STEPS - 1)(lambda: result(k).start())

    def result(k):
        span = pl.ds(k * PLANES, PLANES)
        return pltpu.make_async_copy(dens.at[span], out.at[0, span], out_sem.at[k])

    load_density = pltpu.make_async_copy(phonons.at[0], dens.at[pl.ds(0, planes)], load_sem.at[4])
    load_density.start()
    order = (me, inward, jnp.clip(outward, 0, 3), far)
    loads = [
        pltpu.make_async_copy(
            coupling.at[:, pl.ds(pl.multiple_of(block * width, width), width)], weights.at[j], load_sem.at[j]
        )
        for j, block in enumerate(order)
    ]
    for load in loads:
        load.start()

    barrier = pltpu.get_barrier_semaphore()

    def greet(c, m):
        pl.semaphore_signal(barrier, inc=1, device_id=(c, m), device_id_type=MESH)

    greet(cell, inward)
    pl.when(is_inner)(lambda: greet(cell, outward))
    for c in (y_next, y_last, x_next, x_last, twin) + peers:
        greet(c, me)
    pl.semaphore_wait(barrier, 9 + inner)

    @pl.when(jnp.logical_not(is_inner))
    def _():
        lent_z(0).start()
        lent_z(1).start()

    load_density.wait()

    @pl.loop(0, count)
    def _(i):
        own[i] = dens[pl.ds(i * PLANES, PLANES)].astype(jnp.bfloat16)
        on_own_sends(i, lambda copy: copy.start())

    for load in loads:
        load.wait()

    @pl.loop(0, steps_all + 1)
    def _(t):
        @pl.when(is_inner)
        def _():
            @pl.when(t < steps_all)
            def _():
                arrived(1, t)
                relay(t).start()

            @pl.when(t == LENT_AT - 3)
            def _():
                for k in range(2):
                    lent_z(k).wait_recv()
                for q, k in pairs:
                    lent_peer(q, k).start()

            @pl.when(t == LENT_AT - 1)
            def _():
                for q, k in pairs:
                    lent_peer(q, k).wait_recv()
                for q, k in twins:
                    lent_twin(q, k).start()

        @pl.when(t >= 1)
        def _():
            u = t - 1
            process(u)

            @pl.when(is_inner)
            def _():
                @pl.when(u == LENT_AT)
                def _():
                    for q, k in twins:
                        lent_twin(q, k).wait_recv()
                    pl.loop(0, LENT_AT)(partial_sum)

                pl.when(u >= LENT_AT)(lambda: partial_sum(u))

    @pl.loop(0, count)
    def _(k):
        result(k).wait()

    @pl.when(is_inner)
    def _():
        pl.loop(0, steps_all)(lambda i: part(i).wait_send())
        for q, k in pairs:
            lent_peer(q, k).wait_send()
        for q, k in twins:
            lent_twin(q, k).wait_send()

    @pl.when(jnp.logical_not(is_inner))
    def _():
        lent_z(0).wait_send()
        lent_z(1).wait_send()


def line_device(phonons, heaters, courant, upwind, relaxation, source, coupling):
    _, planes, ny, nz, width = phonons.shape
    count = planes // PLANES
    calls = STEPS * count
    forward = (upwind == 1).astype(jnp.float32)
    behind, ahead = courant * forward, courant * (1.0 - forward)
    stay = 1.0 - courant[0] - courant[1] - courant[2] - relaxation
    rates = jnp.stack([stay, behind[0], ahead[0], behind[1], ahead[1], behind[2], ahead[2], source])
    heat = heaters[0].astype(jnp.float32).reshape(planes, ny * nz, 1)
    anywhere, vmem = pl.BlockSpec(memory_space=pl.ANY), pl.BlockSpec(memory_space=pltpu.VMEM)
    dma = pltpu.SemaphoreType.DMA
    half, full = jnp.bfloat16, jnp.float32
    return pl.pallas_call(
        line_kernel,
        out_shape=jax.ShapeDtypeStruct(phonons.shape, full),
        in_specs=[anywhere, vmem, vmem, anywhere],
        out_specs=anywhere,
        scratch_shapes=[
            pltpu.VMEM((planes + 1, ny, nz, width), full),
            pltpu.VMEM((count, PLANES, ny, nz, width), half),
            pltpu.VMEM((3, calls, PLANES, ny, nz, width), half),
            pltpu.VMEM((6, width, width), half),
            pltpu.VMEM((2, ny + 2, nz, width), full),
            pltpu.VMEM((2, STEPS, ny, nz, width), half),
            pltpu.VMEM((2, calls, PLANES, nz, width), half),
            pltpu.VMEM((PLANES * ny * nz, width), full),
            dma((5,)),
            dma((4, calls)),
            dma((3, calls)),
            dma((2, calls)),
            dma((2, calls)),
            dma((2, STEPS)),
            dma((2, STEPS)),
            dma((16,)),
            dma((16,)),
            dma((count,)),
        ],
        compiler_params=pltpu.CompilerParams(
            collective_id=0, has_side_effects=True, vmem_limit_bytes=64 * 2**20 - 2**18
        ),
    )(phonons, heat, rates, coupling)


def shifted(block, axis, distance):
    devices = range(lax.axis_size(axis))
    route = [((i - distance) % len(devices), i) for i in devices]
    return lax.ppermute(block, axis, route)


def upstream(density, forward, axis):
    widths = [(0, 0)] * density.ndim
    widths[axis] = (1, 1)
    padded = jnp.pad(density, widths)
    length_axis = density.shape[axis]
    behind = lax.slice_in_dim(padded, 0, length_axis, axis=axis)
    ahead = lax.slice_in_dim(padded, 2, length_axis + 2, axis=axis)
    return jnp.where(forward, behind, ahead)


def scatter_term(rounded, coupling):
    contract = (((1,), (1,)), ((), ()))
    gathered = lax.all_gather(rounded, "modes", axis=1, tiled=True)
    return lax.dot_general(gathered, coupling, contract, preferred_element_type=jnp.float32)


def advect(density, courant, upwind, masks):
    lower_y_ok, upper_y_ok = masks
    forward_x = upwind[0] == 1
    forward_y = upwind[1] == 1
    forward_z = upwind[2] == 1
    below_x = shifted(density[-1].astype(jnp.bfloat16), "cells", GY).astype(jnp.float32)
    above_x = shifted(density[0], "cells", -GY)
    below_y = (
        shifted(density[:, -1].astype(jnp.bfloat16), "cells", 1).astype(jnp.float32) * lower_y_ok
    )
    above_y = (
        shifted(density[:, 0].astype(jnp.bfloat16), "cells", -1).astype(jnp.float32) * upper_y_ok
    )
    upstream_z = upstream(density, forward_z, 2)
    transport = courant[0] * (density - upstream(density, forward_x, 0))
    transport = transport + courant[1] * (density - upstream(density, forward_y, 1))
    transport = transport + courant[2] * (density - upstream_z)
    transport = transport.at[0].add(-courant[0] * jnp.where(forward_x, below_x, 0.0))
    transport = transport.at[-1].add(-courant[0] * jnp.where(forward_x, 0.0, above_x))
    transport = transport.at[:, 0].add(-courant[1] * jnp.where(forward_y, below_y, 0.0))
    transport = transport.at[:, -1].add(-courant[1] * jnp.where(forward_y, 0.0, above_y))
    return transport


def per_device(phonons, heaters, courant, upwind, relaxation, source, coupling):
    density = phonons[0]
    cell_count = density.shape[0] * density.shape[1] * density.shape[2]
    mode_count = density.shape[3]
    block_total = lax.axis_size("cells")
    position = (lax.axis_index("cells") + 2) % block_total
    column = position % GY
    masks = ((column != 0).astype(jnp.float32), (column != GY - 1).astype(jnp.float32))
    heating = heaters[0].astype(jnp.float32)[..., None] * source
    for repeat in range(STEPS):
        rounded = density.astype(jnp.bfloat16).reshape(cell_count, mode_count)
        scattered = scatter_term(rounded, coupling).reshape(density.shape)
        transport = advect(density, courant, upwind, masks)
        density = density - transport - relaxation * density - scattered + heating
    return density[None]


def solution(mesh):
    placed = (
        P("cells", None, None, None, "modes"),
        P("cells", None, None, None),
        P(None, "modes"),
        P(None, "modes"),
        P("modes"),
        P("modes"),
        P("modes", None),
    )
    on_line = mesh.shape["modes"] == 4 and mesh.shape["cells"] == 8
    return jax.shard_map(
        line_device if on_line else per_device,
        mesh=mesh,
        in_specs=placed,
        out_specs=P("cells", None, None, None, "modes"),
        check_vma=False,
    )
```

```python
import jax
import jax.numpy as jnp
from jax import lax
from jax.experimental import pallas as pl
from jax.experimental.pallas import tpu as pltpu
from jax.sharding import PartitionSpec as P

GY = 4
STEPS = 2

PLANES = 1
TILE = 768
LENT_FROM, LENT_TWIN, LENT_AT = 0, 3, 4
MESH = pl.DeviceIdType.MESH


def line_kernel(phonons, heat, rates, coupling, out, dens, own, got, weights, old, facex, facey, total,
                load_sem, ss, rs, fys, fyr, fxs, fxr, hs, hr, out_sem):
    cell, me = lax.axis_index("cells"), lax.axis_index("modes")
    count = own.shape[0]
    steps_all = STEPS * count
    planes = count * PLANES
    ny, nz, width = own.shape[2:]
    rows = PLANES * ny * nz
    blocks = lax.axis_size("cells")
    half = me // 2
    inner = lax.rem((me + 1) // 2, 2)
    is_inner = inner == 1
    toward = 1 - 2 * half
    inward, outward = me + toward, me - toward
    near, far = me + 2 * toward, 3 - 3 * half
    y_next, y_last = lax.rem(cell + 1, blocks), lax.rem(cell + blocks - 1, blocks)
    x_next, x_last = lax.rem(cell + GY, blocks), lax.rem(cell + blocks - GY, blocks)
    twin = cell + 1 - 2 * lax.rem(cell, 2)
    flip2 = 2 - 4 * lax.rem(cell // 2, 2)
    flip4 = 4 - 8 * lax.rem(cell // 4, 2)
    peers = (cell + flip2, cell + flip4, cell + flip2 + flip4)
    column = lax.rem(lax.rem(cell + 2, blocks), GY)
    low_ok = jnp.where(column != 0, 1.0, 0.0).astype(jnp.float32)
    high_ok = jnp.where(column != GY - 1, 1.0, 0.0).astype(jnp.float32)

    def remote(src, dst, send, recv, c, m):
        return pltpu.make_async_remote_copy(
            src_ref=src, dst_ref=dst, send_sem=send, recv_sem=recv, device_id=(c, m), device_id_type=MESH
        )

    def own_in(i):
        return remote(own.at[lax.rem(i, count)], got.at[1 - inner, i], ss.at[0, i], rs.at[1 - inner, i], cell, inward)

    def own_out(i):
        return remote(own.at[lax.rem(i, count)], got.at[0, i], ss.at[1, i], rs.at[0, i], cell, outward)

    def relay(i):
        return remote(got.at[1, i], got.at[2, i], ss.at[2, i], rs.at[2, i], cell, inward)

    def part(i):
        return remote(got.at[1, i], got.at[2, i], ss.at[3, i], rs.at[2, i], cell, outward)

    def arrived(slot, i):
        remote(got.at[slot, i], got.at[slot, i], ss.at[0, i], rs.at[slot, i], cell, inward).wait_recv()

    def face_y(side, i):
        line = own.at[lax.rem(i, count), :, ny - 1 if side == 0 else 0]
        return remote(line, facey.at[side, i], fys.at[side, i], fyr.at[side, i], y_next if side == 0 else y_last, me)

    def face_x(side, s):
        plane = own.at[count - 1, PLANES - 1] if side == 0 else own.at[0, 0]
        return remote(plane, facex.at[side, s], fxs.at[side, s], fxr.at[side, s], x_next if side == 0 else x_last, me)

    share = width // blocks

    def lent_rows(c):
        return pl.ds(pl.multiple_of(c * share, share), share)

    def lent_z(k):
        block = near if k == 0 else far
        src = coupling.at[lent_rows(cell), pl.ds(pl.multiple_of(block * width, width), width)]
        return remote(src, weights.at[4 + k, lent_rows(cell)], hs.at[k], hr.at[k], cell, inward)

    def lent_peer(q, k):
        piece = weights.at[4 + k, lent_rows(cell)]
        return remote(piece, piece, hs.at[2 + 2 * q + k], hr.at[2 + 2 * q + k], peers[q], me)

    def lent_twin(q, k):
        piece = weights.at[4 + k, lent_rows(cell if q == 3 else peers[q])]
        return remote(piece, piece, hs.at[8 + 2 * q + k], hr.at[8 + 2 * q + k], twin, me)

    pairs = [(q, k) for q in range(3) for k in range(2)]
    twins = [(q, k) for q in range(4) for k in range(2)]

    def on_own_sends(i, act):
        act(own_in(i))
        pl.when(is_inner)(lambda: act(own_out(i)))
        act(face_y(0, i))
        act(face_y(1, i))
        pl.when(lax.rem(i, count) == 0)(lambda: act(face_x(1, i // count)))
        pl.when(lax.rem(i, count) == count - 1)(lambda: act(face_x(0, i // count)))

    def matrix(piece):
        return piece[...].reshape(rows, width)

    def product(piece, block, tile):
        weight = weights[block, pl.ds(pl.multiple_of(tile * TILE, TILE), TILE), :]
        return lax.dot_general(matrix(piece), weight, (((1,), (1,)), ((), ())), preferred_element_type=jnp.float32)

    def add_product(piece, block, first=False):
        @pl.loop(0, width // TILE)
        def _(tile):
            lanes = pl.ds(pl.multiple_of(tile * TILE, TILE), TILE)
            value = product(piece, block, tile)
            total[:, lanes] = value if first else total[:, lanes] + value

    def partial_sum(i):
        relay(i).wait_send()

        @pl.loop(0, width // TILE)
        def _(tile):
            lanes = pl.ds(pl.multiple_of(tile * TILE, TILE), TILE)
            value = product(got.at[0, i], 4, tile) + product(got.at[2, i], 5, tile)
            got[1, i, :, :, :, lanes] = value.astype(jnp.bfloat16).reshape(PLANES, ny, nz, TILE)

        part(i).start()

    def process(i):
        s, k = i // count, lax.rem(i, count)
        add_product(own.at[k], 0, True)
        arrived(0, i)
        add_product(got.at[0, i], 1)
        pl.when(is_inner)(lambda: add_product(got.at[1, i], 2))
        arrived(2, i)
        pl.when(is_inner)(lambda: add_product(got.at[2, i], 3))

        @pl.when(jnp.logical_not(is_inner))
        def _():
            total[...] = total[...] + got[2, i].reshape(rows, width).astype(jnp.float32)

        face_y(0, i).wait_recv()
        face_y(1, i).wait_recv()

        @pl.when(k == 0)
        def _():
            face_x(0, s).wait_recv()
            old[1, 1 : ny + 1] = facex[0, s].astype(jnp.float32)

        @pl.when(k == count - 1)
        def _():
            face_x(1, s).wait_recv()
            dens[planes] = facex[1, s].astype(jnp.float32)

        on_own_sends(i, lambda copy: copy.wait_send())
        spot = lax.broadcasted_iota(jnp.int32, (nz, 512), 0)
        for p in range(PLANES):
            plane = k * PLANES + p
            cur = lax.rem(plane, 2)
            old[cur, 1 : ny + 1] = dens[plane]
            old[cur, 0] = facey[0, i, p].astype(jnp.float32) * low_ok
            old[cur, ny + 1] = facey[1, i, p].astype(jnp.float32) * high_ok

            @pl.loop(0, ny)
            def _(y):
                warm = heat[plane, pl.ds(pl.multiple_of(y * nz, nz), nz), :]
                for lane in range(0, width, 512):
                    lanes = slice(lane, lane + 512)
                    here = old[cur, y + 1, :, lanes]
                    new = rates[0:1, lanes] * here
                    new += rates[1:2, lanes] * old[1 - cur, y + 1, :, lanes]
                    new += rates[2:3, lanes] * dens[plane + 1, y, :, lanes]
                    new += rates[3:4, lanes] * old[cur, y, :, lanes]
                    new += rates[4:5, lanes] * old[cur, y + 2, :, lanes]
                    new += rates[5:6, lanes] * jnp.where(spot == 0, 0.0, pltpu.roll(here, 1, 0))
                    new += rates[6:7, lanes] * jnp.where(spot == nz - 1, 0.0, pltpu.roll(here, nz - 1, 0))
                    line = pl.ds(pl.multiple_of((p * ny + y) * nz, nz), nz)
                    new += warm * rates[7:8, lanes] - total[line, lanes]
                    dens[plane, y, :, lanes] = new
                    own[k, p, y, :, lanes] = new.astype(jnp.bfloat16)

        pl.when(s < STEPS - 1)(lambda: on_own_sends(i + count, lambda copy: copy.start()))
        pl.when(s == STEPS - 1)(lambda: result(k).start())

    def result(k):
        span = pl.ds(k * PLANES, PLANES)
        return pltpu.make_async_copy(dens.at[span], out.at[0, span], out_sem.at[k])

    load_density = pltpu.make_async_copy(phonons.at[0], dens.at[pl.ds(0, planes)], load_sem.at[4])
    load_density.start()
    order = (me, inward, jnp.clip(outward, 0, 3), far)
    loads = [
        pltpu.make_async_copy(
            coupling.at[:, pl.ds(pl.multiple_of(block * width, width), width)], weights.at[j], load_sem.at[j]
        )
        for j, block in enumerate(order)
    ]
    for load in loads:
        load.start()

    barrier = pltpu.get_barrier_semaphore()

    def greet(c, m):
        pl.semaphore_signal(barrier, inc=1, device_id=(c, m), device_id_type=MESH)

    greet(cell, inward)
    pl.when(is_inner)(lambda: greet(cell, outward))
    for c in (y_next, y_last, x_next, x_last, twin) + peers:
        greet(c, me)
    pl.semaphore_wait(barrier, 9 + inner)

    @pl.when(jnp.logical_not(is_inner))
    def _():
        lent_z(0).start()
        lent_z(1).start()
        lent_z(0).wait_send()
        lent_z(1).wait_send()

    load_density.wait()

    @pl.loop(0, count)
    def _(i):
        own[i] = dens[pl.ds(i * PLANES, PLANES)].astype(jnp.bfloat16)
        on_own_sends(i, lambda copy: copy.start())

    for load in loads:
        load.wait()

    @pl.loop(0, steps_all + 1)
    def _(t):
        @pl.when(is_inner)
        def _():
            @pl.when(t == LENT_FROM)
            def _():
                for k in range(2):
                    lent_z(k).wait_recv()
                for q, k in pairs:
                    lent_peer(q, k).start()

            @pl.when(t == LENT_TWIN)
            def _():
                for q, k in pairs:
                    lent_peer(q, k).wait_recv()
                for q, k in twins:
                    lent_twin(q, k).start()

            @pl.when(t < steps_all)
            def _():
                arrived(1, t)
                relay(t).start()

        @pl.when(t >= 1)
        def _():
            u = t - 1
            process(u)

            @pl.when(is_inner)
            def _():
                @pl.when(u == LENT_AT)
                def _():
                    for q, k in twins:
                        lent_twin(q, k).wait_recv()
                    pl.loop(0, LENT_AT)(partial_sum)

                pl.when(u >= LENT_AT)(lambda: partial_sum(u))

    @pl.loop(0, count)
    def _(k):
        result(k).wait()

    @pl.when(is_inner)
    def _():
        pl.loop(0, steps_all)(lambda i: part(i).wait_send())
        for q, k in pairs:
            lent_peer(q, k).wait_send()
        for q, k in twins:
            lent_twin(q, k).wait_send()


def line_device(phonons, heaters, courant, upwind, relaxation, source, coupling):
    _, planes, ny, nz, width = phonons.shape
    count = planes // PLANES
    calls = STEPS * count
    forward = (upwind == 1).astype(jnp.float32)
    behind, ahead = courant * forward, courant * (1.0 - forward)
    stay = 1.0 - courant[0] - courant[1] - courant[2] - relaxation
    rates = jnp.stack([stay, behind[0], ahead[0], behind[1], ahead[1], behind[2], ahead[2], source])
    heat = heaters[0].astype(jnp.float32).reshape(planes, ny * nz, 1)
    anywhere, vmem = pl.BlockSpec(memory_space=pl.ANY), pl.BlockSpec(memory_space=pltpu.VMEM)
    dma = pltpu.SemaphoreType.DMA
    half, full = jnp.bfloat16, jnp.float32
    return pl.pallas_call(
        line_kernel,
        out_shape=jax.ShapeDtypeStruct(phonons.shape, full),
        in_specs=[anywhere, vmem, vmem, anywhere],
        out_specs=anywhere,
        scratch_shapes=[
            pltpu.VMEM((planes + 1, ny, nz, width), full),
            pltpu.VMEM((count, PLANES, ny, nz, width), half),
            pltpu.VMEM((3, calls, PLANES, ny, nz, width), half),
            pltpu.VMEM((6, width, width), half),
            pltpu.VMEM((2, ny + 2, nz, width), full),
            pltpu.VMEM((2, STEPS, ny, nz, width), half),
            pltpu.VMEM((2, calls, PLANES, nz, width), half),
            pltpu.VMEM((PLANES * ny * nz, width), full),
            dma((5,)),
            dma((4, calls)),
            dma((3, calls)),
            dma((2, calls)),
            dma((2, calls)),
            dma((2, STEPS)),
            dma((2, STEPS)),
            dma((16,)),
            dma((16,)),
            dma((count,)),
        ],
        compiler_params=pltpu.CompilerParams(
            collective_id=0, has_side_effects=True, vmem_limit_bytes=64 * 2**20 - 2**18
        ),
    )(phonons, heat, rates, coupling)


def shifted(block, axis, distance):
    devices = range(lax.axis_size(axis))
    route = [((i - distance) % len(devices), i) for i in devices]
    return lax.ppermute(block, axis, route)


def upstream(density, forward, axis):
    widths = [(0, 0)] * density.ndim
    widths[axis] = (1, 1)
    padded = jnp.pad(density, widths)
    length_axis = density.shape[axis]
    behind = lax.slice_in_dim(padded, 0, length_axis, axis=axis)
    ahead = lax.slice_in_dim(padded, 2, length_axis + 2, axis=axis)
    return jnp.where(forward, behind, ahead)


def scatter_term(rounded, coupling):
    contract = (((1,), (1,)), ((), ()))
    gathered = lax.all_gather(rounded, "modes", axis=1, tiled=True)
    return lax.dot_general(gathered, coupling, contract, preferred_element_type=jnp.float32)


def advect(density, courant, upwind, masks):
    lower_y_ok, upper_y_ok = masks
    forward_x = upwind[0] == 1
    forward_y = upwind[1] == 1
    forward_z = upwind[2] == 1
    below_x = shifted(density[-1].astype(jnp.bfloat16), "cells", GY).astype(jnp.float32)
    above_x = shifted(density[0], "cells", -GY)
    below_y = (
        shifted(density[:, -1].astype(jnp.bfloat16), "cells", 1).astype(jnp.float32) * lower_y_ok
    )
    above_y = (
        shifted(density[:, 0].astype(jnp.bfloat16), "cells", -1).astype(jnp.float32) * upper_y_ok
    )
    upstream_z = upstream(density, forward_z, 2)
    transport = courant[0] * (density - upstream(density, forward_x, 0))
    transport = transport + courant[1] * (density - upstream(density, forward_y, 1))
    transport = transport + courant[2] * (density - upstream_z)
    transport = transport.at[0].add(-courant[0] * jnp.where(forward_x, below_x, 0.0))
    transport = transport.at[-1].add(-courant[0] * jnp.where(forward_x, 0.0, above_x))
    transport = transport.at[:, 0].add(-courant[1] * jnp.where(forward_y, below_y, 0.0))
    transport = transport.at[:, -1].add(-courant[1] * jnp.where(forward_y, 0.0, above_y))
    return transport


def per_device(phonons, heaters, courant, upwind, relaxation, source, coupling):
    density = phonons[0]
    cell_count = density.shape[0] * density.shape[1] * density.shape[2]
    mode_count = density.shape[3]
    block_total = lax.axis_size("cells")
    position = (lax.axis_index("cells") + 2) % block_total
    column = position % GY
    masks = ((column != 0).astype(jnp.float32), (column != GY - 1).astype(jnp.float32))
    heating = heaters[0].astype(jnp.float32)[..., None] * source
    for repeat in range(STEPS):
        rounded = density.astype(jnp.bfloat16).reshape(cell_count, mode_count)
        scattered = scatter_term(rounded, coupling).reshape(density.shape)
        transport = advect(density, courant, upwind, masks)
        density = density - transport - relaxation * density - scattered + heating
    return density[None]


def solution(mesh):
    placed = (
        P("cells", None, None, None, "modes"),
        P("cells", None, None, None),
        P(None, "modes"),
        P(None, "modes"),
        P("modes"),
        P("modes"),
        P("modes", None),
    )
    on_line = mesh.shape["modes"] == 4 and mesh.shape["cells"] == 8
    return jax.shard_map(
        line_device if on_line else per_device,
        mesh=mesh,
        in_specs=placed,
        out_specs=P("cells", None, None, None, "modes"),
        check_vma=False,
    )
```
